32 devices in a mesh: clip: 2 (over x), tm: 16 (over z, y, core).
Axes of the slice: x: 2, y: 2, z: 4, core: 2. Of those that a mesh axis runs over, the one named last changes fastest.
Arguments:
- tokens: bfloat16 [32768, 512], P(('clip', 'tm')), parts along dimension 0, may hold values from -6 to 6
- qkv_weight: bfloat16 [512, 1536], replicated, may hold values from -0.25 to 0.25
- out_weight: bfloat16 [512, 1024], replicated, may hold values from -0.25 to 0.25
- conv_weight: bfloat16 [3, 3, 256, 256], replicated, may hold values from -0.125 to 0.125
- norm_gain: float32 [256], replicated, may hold values from 0.25 to 1.75
- norm_bias: float32 [256], replicated, may hold values from -3 to 3
- group_map: int32 [32], P('clip'), parts along dimension 0, may hold values from 0 to 7, as said below
- token_order: int32 [2048], P('clip'), parts along dimension 0, may hold values from 0 to 1023, each once
- valid_frames: int32 [32], P('clip'), parts along dimension 0, may hold values from 1 to 16
Outputs:
- decoded: bfloat16 [32, 32, 128, 256], P('clip', 'tm'), parts along dimension 0
The draws below stay inside these ranges and needn't reach their ends.
There are 2 independent parts, one for each index of `clip`. The reference program is written for one: setup_inputs(seed, part) draws one part's arguments, and reference() takes and returns one part's arrays. A program takes and returns all parts, laid end to end along the dimension named above; an argument that names none is the same for every part. Nothing has to cross between parts.
Inputs may be any that keep to these rules, and one draw needn't show every extreme that they name: `group_map`: never falls from one run to the next, and every group from 0 to 7 holds at least one run.
All inputs are finite; a program needn't handle non-finite values.
Results may differ from the reference program's by a relative error of at most 0.0055.
The reference program's roundings to bfloat16 on the way count: a program that leaves them out, or rounds other values in their place, can miss the bound.
Values may be sent and summed in bfloat16 or wider, within the bound.
A program may use at most 64 MiB of HBM per device.

```python
import jax
import jax.numpy as jnp
from jax import lax

D = 512
HEADS = 16
C = 256
NORM_GROUPS = 32
TIME_GROUPS = 8
TOK_DEV = 1024
TOKENS = 16384
FRAMES = 16
N_TM = 16


def draw_group_map(key, part):
    cuts = jax.random.permutation(jax.random.fold_in(key, 11), N_TM - 1)[:TIME_GROUPS - 1] + 1
    positions = jnp.arange(N_TM, dtype=jnp.int32)
    return jnp.sum((positions[:, None] >= cuts[None, :]).astype(jnp.int32), axis=1).astype(jnp.int32)


def draw_valid_frames(key, part):
    lowest = FRAMES // 3
    positions = jnp.arange(N_TM, dtype=jnp.int32)
    trend = lowest + positions * (FRAMES - lowest) // max(N_TM - 1, 1)
    spread = FRAMES // 8
    jitter = jax.random.randint(jax.random.fold_in(key, 23), (N_TM,), -spread, spread + 1)
    return jnp.clip(trend + jitter, 1, FRAMES).astype(jnp.int32)


def levels(rng, dims, split, smallest, high):
    level = 1.0
    for dim, blocks in split:
        heights = jax.random.uniform(jax.random.fold_in(jax.random.fold_in(rng, 6), dim), (blocks,), jnp.float32, smallest / len(split), high / len(split))
        level = level * jnp.repeat(jnp.exp(heights), dims[dim] // blocks).reshape((-1,) + (1,) * (len(dims) - 1 - dim))
    return level


def gaussian(rng, dims, deviation, bound, pieces=(), held_as=jnp.bfloat16):
    level = levels(rng, dims, pieces, -0.22, 0.18) if pieces else 1.0
    result = jax.random.normal(rng, dims, jnp.float32) * deviation * level
    return jnp.minimum(jnp.maximum(result, -bound), bound).astype(held_as)


def setup_inputs(seed: int = 0, part: int = 0) -> dict:
    arg_keys = jax.random.split(jax.random.key(seed), 10)
    part_keys = jax.random.split(jax.random.fold_in(arg_keys[9], part), 10)
    tokens = gaussian(part_keys[0], (TOKENS, D), 1.0, 6.0, ((0, 16),))
    qkv_weight = gaussian(arg_keys[1], (D, 3 * D), D ** -0.5, 0.25)
    out_weight = gaussian(arg_keys[2], (D, 4 * C), D ** -0.5, 0.25)
    conv_weight = gaussian(arg_keys[3], (3, 3, C, C), (9 * C) ** -0.5, 0.125)
    norm_gain = jnp.clip(1.0 + 0.15 * jax.random.normal(arg_keys[4], (C,), jnp.float32), 0.25, 1.75)
    norm_bias = gaussian(arg_keys[5], (C,), 0.5, 3.0, (), jnp.float32)
    group_map = draw_group_map(jax.random.fold_in(jax.random.fold_in(arg_keys[9], part), 71), part)
    token_order = jax.random.permutation(part_keys[7], TOK_DEV).astype(jnp.int32)
    valid_frames = draw_valid_frames(jax.random.fold_in(jax.random.fold_in(arg_keys[9], part), 71), part)
    return dict(tokens=tokens, qkv_weight=qkv_weight, out_weight=out_weight, conv_weight=conv_weight, norm_gain=norm_gain, norm_bias=norm_bias, group_map=group_map, token_order=token_order, valid_frames=valid_frames)


def reference(tokens, qkv_weight, out_weight, conv_weight, norm_gain, norm_bias, group_map, token_order, valid_frames):
    head_dim = D // HEADS
    highest = lax.Precision.HIGHEST
    spans = tokens.reshape(N_TM, TOK_DEV, D)

    def span_state(span):
        mixed = jnp.dot(span, qkv_weight, preferred_element_type=jnp.float32).astype(jnp.bfloat16)
        key_feats = jax.nn.relu(mixed[:, D:2 * D]).astype(jnp.float32).reshape(TOK_DEV, HEADS, head_dim)
        value_rows = mixed[:, 2 * D:].astype(jnp.float32).reshape(TOK_DEV, HEADS, head_dim)
        state = jnp.einsum('thk,thv->khv', key_feats, value_rows, precision=highest).reshape(head_dim, D)
        return (state, lax.optimization_barrier(jnp.sum(key_feats, axis=0)).reshape(D))
    span_states, span_sums = lax.map(span_state, spans)
    earlier = (group_map[None, :] < group_map[:, None]).astype(jnp.float32)
    prefix_states = jnp.einsum('cd,dkv->ckv', earlier, span_states, precision=highest)
    prefix_sums = jnp.dot(earlier, span_sums, precision=highest)
    inverse = jnp.argsort(token_order).astype(jnp.int32)

    def span_output(packed):
        span, state, key_total = packed
        mixed = jnp.dot(span, qkv_weight, preferred_element_type=jnp.float32).astype(jnp.bfloat16)
        query_feats = jax.nn.relu(mixed[:, :D]).astype(jnp.float32).reshape(TOK_DEV, HEADS, head_dim)
        numer = jnp.einsum('thk,khv->thv', query_feats, state.reshape(head_dim, HEADS, head_dim), precision=highest)
        denom = jnp.einsum('thk,hk->th', query_feats, key_total.reshape(HEADS, head_dim), precision=highest) + 1.0
        attended = (numer / denom[:, :, None]).reshape(TOK_DEV, D).astype(jnp.bfloat16)
        raster = jnp.take(attended, inverse, axis=0)
        return jnp.dot(raster, out_weight, preferred_element_type=jnp.float32).astype(jnp.bfloat16)
    mapped = lax.map(span_output, (spans, span_states + prefix_states, span_sums + prefix_sums))
    row_tokens = TOK_DEV // N_TM
    shuffled = mapped.reshape(N_TM, N_TM, row_tokens, 2, 2, C).transpose(0, 1, 3, 2, 4, 5)
    shuffled = shuffled.reshape(N_TM, 2 * N_TM, 2 * row_tokens, C)
    row_tile = jnp.arange(2 * N_TM, dtype=jnp.int32) // 2
    frame_ids = jnp.arange(N_TM, dtype=jnp.int32)
    frame_mask = (frame_ids[:, None] < jnp.take(valid_frames, row_tile)[None, :])[:, :, None, None]
    shuffled = jnp.where(frame_mask, shuffled, jnp.zeros((), jnp.bfloat16))
    convolved = lax.conv_general_dilated(shuffled, conv_weight, (1, 1), ((1, 1), (1, 1)), dimension_numbers=('NHWC', 'HWIO', 'NHWC'), preferred_element_type=jnp.float32)
    convolved = jnp.where(frame_mask, convolved, jnp.zeros((), jnp.float32))
    group_size = C // NORM_GROUPS
    total_count = jnp.sum(valid_frames).astype(jnp.float32) * (group_size * 4 * row_tokens)

    def group_total(field):
        return lax.optimization_barrier(jnp.sum(field, axis=(0, 1, 2))).reshape(NORM_GROUPS, group_size).sum(axis=1)
    group_mean = group_total(convolved) / total_count
    centred = jnp.where(frame_mask, convolved - jnp.repeat(group_mean, group_size), jnp.zeros((), jnp.float32))
    group_var = group_total(centred * centred) / total_count
    norm_scale = norm_gain * lax.rsqrt(jnp.repeat(group_var, group_size) + 1e-05)
    normed = centred * norm_scale + norm_bias
    decoded = jnp.where(frame_mask, jax.nn.silu(normed), jnp.zeros((), jnp.float32))
    return decoded.astype(jnp.bfloat16)
```

```python
import functools

import jax
import jax.numpy as jnp
from jax import lax
from jax.experimental import pallas as pl
from jax.experimental.pallas import tpu as pltpu
from jax.sharding import PartitionSpec as P

HEADS = 16
NORM_GROUPS = 32
MESH = pl.DeviceIdType.MESH
F32 = jnp.float32
BF16 = jnp.bfloat16
CHUNK = 256
BLOCK = 256


def flat(cells):
    frames, rows, width = cells.shape
    if rows % 16 == 0:
        return cells.reshape(frames * rows, width)
    return cells.astype(F32).reshape(frames * rows, width).astype(BF16)


def mega(
    n,
    tokens_hbm,
    qkv_hbm,
    out_hbm,
    conv_hbm,
    gain_ref,
    bias_ref,
    group_ref,
    order_ref,
    valid_ref,
    decoded_hbm,
    tokens_ref,
    qkv_ref,
    outw_ref,
    convw_ref,
    sent_tokens,
    tile_tokens,
    state_acc,
    sum_acc,
    sent_state,
    all_state,
    running,
    prefix,
    rows_ref,
    cells,
    halo,
    conv_acc,
    stat_acc,
    sent_stat,
    all_stat,
    weave,
    out_buf,
    load_sem,
    tok_send,
    tok_recv,
    st_send,
    st_recv,
    halo_send,
    halo_recv,
    stat_send,
    stat_recv,
    store_sem,
):
    me = lax.axis_index("tm")
    count, width = tokens_ref.shape
    row_tokens = count // n
    chunks = count // CHUNK
    frames_per = CHUNK // row_tokens
    head_dim = width // HEADS
    channels = gain_ref.shape[1]
    blocks = width // BLOCK
    heads_per = BLOCK // head_dim
    group_size = channels // NORM_GROUPS

    loads = [
        pltpu.make_async_copy(a, b, load_sem.at[i])
        for i, (a, b) in enumerate(
            [
                (tokens_hbm, tokens_ref),
                (qkv_hbm, qkv_ref),
                (out_hbm, outw_ref),
                (conv_hbm, convw_ref),
            ]
        )
    ]
    for load in loads:
        load.start()

    barrier = pltpu.get_barrier_semaphore()

    @pl.loop(1, n)
    def _(s):
        pl.semaphore_signal(
            barrier, inc=1, device_id={"tm": lax.rem(me + s, n)}, device_id_type=MESH
        )

    def exchange(s, src, dst, send_sem, recv_sem):
        return pltpu.make_async_remote_copy(
            src_ref=src,
            dst_ref=dst,
            send_sem=send_sem.at[s],
            recv_sem=recv_sem.at[s],
            device_id={"tm": lax.rem(me + s, n)},
            device_id_type=MESH,
        )

    def tok_copy(s):
        return exchange(
            s, sent_tokens.at[lax.rem(me + s, n)], tile_tokens.at[me], tok_send, tok_recv
        )

    def state_copy(s):
        return exchange(s, sent_state, all_state.at[me], st_send, st_recv)

    def stat_copy(s):
        return exchange(s, sent_stat, all_stat.at[me], stat_send, stat_recv)

    loads[0].wait()

    @pl.loop(0, chunks)
    def _(c):
        place = lax.broadcasted_iota(jnp.int32, (CHUNK, count), 0) + c * CHUNK
        pick = jnp.where(order_ref[...] == place, 1.0, 0.0).astype(BF16)
        moved = jnp.dot(pick, tokens_ref[...], preferred_element_type=F32)
        sent_tokens[pl.ds(c * frames_per, frames_per)] = moved.reshape(
            frames_per, row_tokens, width
        ).astype(BF16)

    pl.semaphore_wait(barrier, n - 1)

    @pl.loop(1, n)
    def _(s):
        tok_copy(s).start()

    tile_tokens[me] = sent_tokens[me]

    loads[1].wait()
    state_acc[...] = jnp.zeros_like(state_acc)
    sum_acc[...] = jnp.zeros_like(sum_acc)

    @pl.loop(0, chunks)
    def _(c):
        rows = pl.ds(pl.multiple_of(c * CHUNK, CHUNK), CHUNK)
        mixed = jnp.dot(
            tokens_ref[rows, :], qkv_ref[:, width : 3 * width], preferred_element_type=F32
        ).astype(BF16)
        keys = jnp.maximum(mixed[:, :width], jnp.zeros((), BF16))
        sum_acc[...] += keys.astype(F32).reshape(CHUNK // 8, 8, width).sum(axis=0)
        for b in range(blocks):
            lanes = slice(b * BLOCK, (b + 1) * BLOCK)
            state_acc[b] += lax.dot_general(
                keys[:, lanes],
                mixed[:, width + b * BLOCK : width + (b + 1) * BLOCK],
                (((0,), (0,)), ((), ())),
                preferred_element_type=F32,
            )

    head_row = lax.broadcasted_iota(jnp.int32, (BLOCK, BLOCK), 0) // head_dim
    head_col = lax.broadcasted_iota(jnp.int32, (BLOCK, BLOCK), 1) // head_dim
    same_head = head_row == head_col
    for b in range(blocks):
        own = jnp.where(same_head, state_acc[b], 0.0)
        sent_state[0:head_dim, b * BLOCK : (b + 1) * BLOCK] = (
            own.reshape(heads_per, head_dim, BLOCK).sum(axis=0).astype(BF16)
        )
    key_sum = jnp.sum(sum_acc[...], axis=0, keepdims=True)
    high = key_sum.astype(BF16).astype(F32)
    line = lax.broadcasted_iota(jnp.int32, (16, width), 0)
    sent_state[head_dim : head_dim + 16, :] = jnp.where(
        line == 0, high, jnp.where(line == 1, key_sum - high, 0.0)
    ).astype(BF16)

    @pl.loop(1, n)
    def _(s):
        state_copy(s).start()

    all_state[me] = sent_state[...]

    @pl.loop(1, n)
    def _(s):
        tok_copy(s).wait_recv()

    @pl.loop(0, chunks)
    def _(c):
        rows = pl.ds(pl.multiple_of(c * CHUNK, CHUNK), CHUNK)
        mixed = jnp.dot(
            flat(tile_tokens[pl.ds(c * frames_per, frames_per)]),
            qkv_ref[:, 0:width],
            preferred_element_type=F32,
        ).astype(BF16)
        rows_ref[rows, :] = jnp.maximum(mixed, jnp.zeros((), BF16)).astype(F32)

    @pl.loop(1, n)
    def _(s):
        state_copy(s).wait_recv()

    running[...] = jnp.zeros_like(running)
    prefix[...] = jnp.zeros_like(prefix)
    head_ones = same_head.astype(F32).astype(BF16)

    @pl.loop(0, n)
    def _(f):
        new_group = group_ref[f] != group_ref[jnp.maximum(f - 1, 0)]
        before = jnp.where(new_group, running[...], prefix[...])
        prefix[...] = before
        own = all_state[f].astype(F32)
        running[...] += own
        total = before + own
        state = total[0:head_dim, :]
        key_total = jnp.sum(total[head_dim:, :], axis=0, keepdims=True)
        rows = pl.ds(pl.multiple_of(f * row_tokens, 8), row_tokens)
        query = rows_ref[rows, :]
        scaled = (query * key_total).astype(BF16)
        query = query.astype(BF16)
        for b in range(blocks):
            lanes = slice(b * BLOCK, (b + 1) * BLOCK)
            spread = jnp.concatenate([state[:, lanes]] * heads_per, axis=0)
            spread = jnp.where(same_head, spread, 0.0).astype(BF16)
            numer = jnp.dot(query[:, lanes], spread, preferred_element_type=F32)
            denom = jnp.dot(scaled[:, lanes], head_ones, preferred_element_type=F32) + 1.0
            rows_ref[rows, lanes] = numer / denom

    valid_rows = valid_ref[me] * row_tokens
    loads[2].wait()

    def widen(even, odd):
        column = lax.rem(lax.broadcasted_iota(jnp.int32, even.shape, 0), row_tokens)
        odd_left = jnp.where(column == 0, 0.0, pltpu.roll(odd, 1, 0))
        even_right = jnp.where(column == row_tokens - 1, 0.0, pltpu.roll(even, CHUNK - 1, 0))
        return [x.astype(BF16) for x in (odd_left, even, odd, even_right)]

    def down_copy(c):
        rows = pl.ds(pl.multiple_of(c * CHUNK, CHUNK), CHUNK)
        return pltpu.make_async_remote_copy(
            src_ref=cells.at[1, rows, channels : 3 * channels],
            dst_ref=halo.at[0, rows, :],
            send_sem=halo_send.at[0, c],
            recv_sem=halo_recv.at[0, c],
            device_id={"tm": lax.rem(me + 1, n)},
            device_id_type=MESH,
        )

    def up_copy(c):
        rows = pl.ds(pl.multiple_of(c * CHUNK, CHUNK), CHUNK)
        return pltpu.make_async_remote_copy(
            src_ref=cells.at[0, rows, channels : 3 * channels],
            dst_ref=halo.at[1, rows, :],
            send_sem=halo_send.at[1, c],
            recv_sem=halo_recv.at[1, c],
            device_id={"tm": lax.rem(me + n - 1, n)},
            device_id_type=MESH,
        )

    @pl.loop(0, chunks)
    def _(c):
        rows = pl.ds(pl.multiple_of(c * CHUNK, CHUNK), CHUNK)
        mapped = jnp.dot(
            rows_ref[rows, :].astype(BF16), outw_ref[...], preferred_element_type=F32
        )
        row = lax.broadcasted_iota(jnp.int32, mapped.shape, 0) + c * CHUNK
        mapped = jnp.where(row < valid_rows, mapped, 0.0)
        for a in range(2):
            even = mapped[:, 2 * a * channels : (2 * a + 1) * channels]
            odd = mapped[:, (2 * a + 1) * channels : (2 * a + 2) * channels]
            for i, part in enumerate(widen(even, odd)):
                cells[a, rows, i * channels : (i + 1) * channels] = part

        @pl.when(me < n - 1)
        def _():
            down_copy(c).start()

        @pl.when(me > 0)
        def _():
            up_copy(c).start()

    @pl.when(me == 0)
    def _():
        halo[0] = jnp.zeros(halo.shape[1:], BF16)

    @pl.when(me == n - 1)
    def _():
        halo[1] = jnp.zeros(halo.shape[1:], BF16)

    loads[3].wait()
    reach = 3 * channels

    @pl.loop(0, chunks)
    def _(c):
        rows = pl.ds(pl.multiple_of(c * CHUNK, CHUNK), CHUNK)
        for r in range(2):
            for b in range(2):
                lanes = slice(b * channels, b * channels + reach)
                conv_acc[r, rows, b * channels : (b + 1) * channels] = jnp.dot(
                    cells[0, rows, lanes], convw_ref[1 - r], preferred_element_type=F32
                ) + jnp.dot(cells[1, rows, lanes], convw_ref[2 - r], preferred_element_type=F32)

    stat_acc[...] = jnp.zeros_like(stat_acc)

    @pl.loop(0, chunks)
    def _(c):
        rows = pl.ds(pl.multiple_of(c * CHUNK, CHUNK), CHUNK)

        @pl.when(me > 0)
        def _():
            down_copy(c).wait_recv()

        @pl.when(me < n - 1)
        def _():
            up_copy(c).wait_recv()

        row = lax.broadcasted_iota(jnp.int32, (CHUNK, channels), 0) + c * CHUNK
        for r in range(2):
            edge = halo[r, rows, :].astype(F32)
            parts = widen(edge[:, :channels], edge[:, channels:])
            for b in range(2):
                taps = jnp.concatenate(parts[b : b + 3], axis=1)
                lanes = slice(b * channels, (b + 1) * channels)
                result = conv_acc[r, rows, lanes] + jnp.dot(
                    taps, convw_ref[2 * r], preferred_element_type=F32
                )
                result = jnp.where(row < valid_rows, result, 0.0)
                conv_acc[r, rows, lanes] = result
                stat_acc[0] += result.reshape(CHUNK // 8, 8, channels).sum(axis=0)

    unit = (4 * row_tokens * group_size)
    group_row = lax.broadcasted_iota(jnp.int32, (channels, channels), 0) // group_size
    group_col = lax.broadcasted_iota(jnp.int32, (channels, channels), 1) // group_size
    group_ones = (group_row == group_col).astype(F32)

    def group_total(part):
        sums = jnp.sum(part, axis=0, keepdims=True)
        return jnp.dot(
            jnp.broadcast_to(sums, (8, channels)),
            group_ones,
            precision=lax.Precision.HIGHEST,
            preferred_element_type=F32,
        )

    tile_sum = group_total(stat_acc[0])
    tile_mean = tile_sum[0:1, :] / (valid_ref[me] * unit).astype(F32)

    @pl.loop(0, chunks)
    def _(c):
        rows = pl.ds(pl.multiple_of(c * CHUNK, CHUNK), CHUNK)
        row = lax.broadcasted_iota(jnp.int32, (CHUNK, channels), 0) + c * CHUNK
        for r in range(2):
            for b in range(2):
                lanes = slice(b * channels, (b + 1) * channels)
                off = jnp.where(row < valid_rows, conv_acc[r, rows, lanes] - tile_mean, 0.0)
                stat_acc[1] += (off * off).reshape(CHUNK // 8, 8, channels).sum(axis=0)

    tile_square = group_total(stat_acc[1])
    line = lax.broadcasted_iota(jnp.int32, (8, channels), 0)
    sent_stat[...] = jnp.where(line == 0, tile_sum, tile_square)

    @pl.loop(1, n)
    def _(s):
        stat_copy(s).start()

    all_stat[me] = sent_stat[...]

    @pl.loop(1, n)
    def _(s):
        stat_copy(s).wait_recv()

    def add_sum(t, carry):
        total, units = carry
        return total + all_stat[t, 0:1, :], units + valid_ref[t]

    total, units = lax.fori_loop(
        0, n, add_sum, (jnp.zeros((1, channels), F32), jnp.zeros((), jnp.int32))
    )
    total_count = units.astype(F32) * unit
    mean = total / total_count

    def add_square(t, square):
        size = (valid_ref[t] * unit).astype(F32)
        off = all_stat[t, 0:1, :] / size - mean
        return square + all_stat[t, 1:2, :] + size * (off * off)

    square = lax.fori_loop(0, n, add_square, jnp.zeros((1, channels), F32))
    scale = gain_ref[...] * lax.rsqrt(square / total_count + 1e-05)
    shift = bias_ref[...]

    def store(c):
        frames = pl.ds(c * frames_per, frames_per)
        return pltpu.make_async_copy(out_buf.at[frames], decoded_hbm.at[frames], store_sem.at[c])

    @pl.loop(0, chunks)
    def _(c):
        rows = pl.ds(pl.multiple_of(c * CHUNK, CHUNK), CHUNK)
        frames = pl.ds(c * frames_per, frames_per)
        row = lax.broadcasted_iota(jnp.int32, (CHUNK, channels), 0) + c * CHUNK
        for r in range(2):
            for b in range(2):
                lanes = slice(b * channels, (b + 1) * channels)
                normed = (conv_acc[r, rows, lanes] - mean) * scale + shift
                active = jnp.where(row < valid_rows, normed * jax.nn.sigmoid(normed), 0.0)
                for h in range(0, channels, 128):
                    weave[h // 128, pl.ds(b, CHUNK, 2), :] = active[:, h : h + 128]
            for h in range(0, channels, 128):
                out_buf[frames, r, :, h : h + 128] = (
                    weave[h // 128].reshape(frames_per, 2 * row_tokens, 128).astype(BF16)
                )
        store(c).start()

    @pl.loop(0, chunks)
    def _(c):
        store(c).wait()

        @pl.when(me < n - 1)
        def _():
            down_copy(c).wait_send()

        @pl.when(me > 0)
        def _():
            up_copy(c).wait_send()

    @pl.loop(1, n)
    def _(s):
        tok_copy(s).wait_send()
        state_copy(s).wait_send()
        stat_copy(s).wait_send()


def local(
    tokens,
    qkv_weight,
    out_weight,
    conv_weight,
    norm_gain,
    norm_bias,
    group_map,
    token_order,
    valid_frames,
):
    n = lax.axis_size("tm")
    count, width = tokens.shape
    channels = conv_weight.shape[3]
    row_tokens = count // n
    chunks = count // CHUNK
    state_rows = width // HEADS + 16
    anywhere = pl.BlockSpec(memory_space=pl.ANY)
    vmem = pl.BlockSpec(memory_space=pltpu.VMEM)
    smem = pl.BlockSpec(memory_space=pltpu.SMEM)
    dma = pltpu.SemaphoreType.DMA
    return pl.pallas_call(
        functools.partial(mega, n),
        out_shape=jax.ShapeDtypeStruct((n, 2, 2 * row_tokens, channels), BF16),
        in_specs=[anywhere] * 4 + [vmem, vmem, smem, vmem, smem],
        out_specs=anywhere,
        scratch_shapes=[
            pltpu.VMEM((count, width), BF16),
            pltpu.VMEM((width, 3 * width), BF16),
            pltpu.VMEM((width, 4 * channels), BF16),
            pltpu.VMEM((3, 3 * channels, channels), BF16),
            pltpu.VMEM((n, row_tokens, width), BF16),
            pltpu.VMEM((n, row_tokens, width), BF16),
            pltpu.VMEM((width // BLOCK, BLOCK, BLOCK), F32),
            pltpu.VMEM((8, width), F32),
            pltpu.VMEM((state_rows, width), BF16),
            pltpu.VMEM((n, state_rows, width), BF16),
            pltpu.VMEM((state_rows, width), F32),
            pltpu.VMEM((state_rows, width), F32),
            pltpu.VMEM((count, width), F32),
            pltpu.VMEM((2, count, 4 * channels), BF16),
            pltpu.VMEM((2, count, 2 * channels), BF16),
            pltpu.VMEM((2, count, 2 * channels), F32),
            pltpu.VMEM((2, 8, channels), F32),
            pltpu.VMEM((8, channels), F32),
            pltpu.VMEM((n, 8, channels), F32),
            pltpu.VMEM((channels // 128, 2 * CHUNK, 128), F32),
            pltpu.VMEM((n, 2, 2 * row_tokens, channels), BF16),
            dma((4,)),
            dma((n,)),
            dma((n,)),
            dma((n,)),
            dma((n,)),
            dma((2, chunks)),
            dma((2, chunks)),
            dma((n,)),
            dma((n,)),
            dma((chunks,)),
        ],
        compiler_params=pltpu.CompilerParams(
            collective_id=0, has_side_effects=True, vmem_limit_bytes=60 * 1024 * 1024
        ),
    )(
        tokens,
        qkv_weight,
        out_weight,
        conv_weight.reshape(3, 3 * channels, channels),
        norm_gain[None],
        norm_bias[None],
        group_map,
        token_order[None],
        valid_frames,
    )


def solution(mesh):
    in_specs = (P(("clip", "tm"), None), P(), P(), P(), P(), P(), P("clip"), P("clip"), P("clip"))
    out_specs = P("clip", "tm", None, None)
    return jax.shard_map(local, mesh=mesh, in_specs=in_specs, out_specs=out_specs, check_vma=False)
```

```python
import functools

import jax
import jax.numpy as jnp
from jax import lax
from jax.experimental import pallas as pl
from jax.experimental.pallas import tpu as pltpu
from jax.sharding import PartitionSpec as P

HEADS = 16
NORM_GROUPS = 32
MESH = pl.DeviceIdType.MESH
F32 = jnp.float32
BF16 = jnp.bfloat16
CHUNK = 256
BLOCK = 256


def flat(cells):
    frames, rows, width = cells.shape
    if rows % 16 == 0:
        return cells.reshape(frames * rows, width)
    return cells.astype(F32).reshape(frames * rows, width).astype(BF16)


def mega(
    n,
    tokens_hbm,
    qkv_hbm,
    out_hbm,
    conv_hbm,
    gain_ref,
    group_ref,
    order_ref,
    valid_ref,
    conv_out,
    norm_ref,
    tokens_ref,
    qkv_ref,
    outw_ref,
    convw_ref,
    sent_tokens,
    tile_tokens,
    state_acc,
    sum_acc,
    sent_state,
    all_state,
    all_total,
    running,
    prefix,
    rows_ref,
    cells,
    halo,
    conv_acc,
    stat_acc,
    sent_stat,
    all_stat,
    out_buf,
    load_sem,
    tok_send,
    tok_recv,
    st_send,
    st_recv,
    pass_send,
    pass_recv,
    halo_send,
    halo_recv,
    stat_send,
    stat_recv,
    store_sem,
):
    me = lax.axis_index("tm")
    count, width = tokens_ref.shape
    row_tokens = count // n
    chunks = count // CHUNK
    frames_per = CHUNK // row_tokens
    head_dim = width // HEADS
    channels = gain_ref.shape[1]
    blocks = width // BLOCK
    heads_per = BLOCK // head_dim
    group_size = channels // NORM_GROUPS

    loads = [
        pltpu.make_async_copy(a, b, load_sem.at[i])
        for i, (a, b) in enumerate(
            [
                (tokens_hbm, tokens_ref),
                (qkv_hbm, qkv_ref),
                (out_hbm, outw_ref),
                (conv_hbm, convw_ref),
            ]
        )
    ]
    for load in loads:
        load.start()

    barrier = pltpu.get_barrier_semaphore()

    @pl.loop(1, n)
    def _(s):
        pl.semaphore_signal(
            barrier, inc=1, device_id={"tm": lax.rem(me + s, n)}, device_id_type=MESH
        )

    def exchange(s, src, dst, send_sem, recv_sem):
        return pltpu.make_async_remote_copy(
            src_ref=src,
            dst_ref=dst,
            send_sem=send_sem.at[s],
            recv_sem=recv_sem.at[s],
            device_id={"tm": lax.rem(me + s, n)},
            device_id_type=MESH,
        )

    def tok_copy(t):
        return pltpu.make_async_remote_copy(
            src_ref=sent_tokens.at[t],
            dst_ref=tile_tokens.at[me],
            send_sem=tok_send.at[t],
            recv_sem=tok_recv.at[me],
            device_id={"tm": t},
            device_id_type=MESH,
        )

    def tok_arrival(t):
        return pltpu.make_async_remote_copy(
            src_ref=sent_tokens.at[t],
            dst_ref=tile_tokens.at[t],
            send_sem=tok_send.at[t],
            recv_sem=tok_recv.at[t],
            device_id={"tm": t},
            device_id_type=MESH,
        )

    partner = me + 1 - 2 * lax.rem(me, 2)

    def state_copy(k):
        return pltpu.make_async_remote_copy(
            src_ref=sent_state,
            dst_ref=all_state.at[me],
            send_sem=st_send.at[k],
            recv_sem=st_recv.at[k],
            device_id={"tm": lax.rem(me + 2 * k, n)},
            device_id_type=MESH,
        )

    def state_pass(k):
        source = lax.rem(me + n - 2 * k, n)
        return pltpu.make_async_remote_copy(
            src_ref=all_state.at[source],
            dst_ref=all_state.at[source],
            send_sem=pass_send.at[k],
            recv_sem=pass_recv.at[k],
            device_id={"tm": partner},
            device_id_type=MESH,
        )

    own_pass = pltpu.make_async_remote_copy(
        src_ref=sent_state,
        dst_ref=all_state.at[me],
        send_sem=pass_send.at[0],
        recv_sem=pass_recv.at[0],
        device_id={"tm": partner},
        device_id_type=MESH,
    )

    def stat_copy(s):
        return exchange(s, sent_stat, all_stat.at[me], stat_send, stat_recv)

    half = chunks // 2
    near = lax.div(me, n // 2) * half
    far = half - near

    loads[0].wait()
    loads[1].wait()
    state_acc[...] = jnp.zeros_like(state_acc)
    sum_acc[...] = jnp.zeros_like(sum_acc)

    @pl.loop(0, chunks)
    def _(c):
        rows = pl.ds(pl.multiple_of(c * CHUNK, CHUNK), CHUNK)
        mixed = jnp.dot(
            tokens_ref[rows, :], qkv_ref[:, width : 3 * width], preferred_element_type=F32
        ).astype(BF16)
        keys = jnp.maximum(mixed[:, :width], jnp.zeros((), BF16))
        sum_acc[...] += keys.astype(F32).reshape(CHUNK // 8, 8, width).sum(axis=0)
        for b in range(blocks):
            lanes = slice(b * BLOCK, (b + 1) * BLOCK)
            state_acc[b] += lax.dot_general(
                keys[:, lanes],
                mixed[:, width + b * BLOCK : width + (b + 1) * BLOCK],
                (((0,), (0,)), ((), ())),
                preferred_element_type=F32,
            )

    head_row = lax.broadcasted_iota(jnp.int32, (BLOCK, BLOCK), 0) // head_dim
    head_col = lax.broadcasted_iota(jnp.int32, (BLOCK, BLOCK), 1) // head_dim
    same_head = head_row == head_col
    pieces = width // 128
    for b in range(blocks):
        own = jnp.where(same_head, state_acc[b], 0.0)
        own = own.reshape(heads_per, head_dim, BLOCK).sum(axis=0).astype(BF16)
        for i in range(BLOCK // 128):
            at = (b * (BLOCK // 128) + i) * head_dim
            sent_state[at : at + head_dim, :] = own[:, i * 128 : (i + 1) * 128]
    key_sum = jnp.sum(sum_acc[...], axis=0, keepdims=True)
    high = key_sum.astype(BF16).astype(F32)
    line = lax.broadcasted_iota(jnp.int32, (16, 128), 0)
    packed = jnp.zeros((16, 128), F32)
    for i in range(pieces):
        lanes = slice(i * 128, (i + 1) * 128)
        packed = jnp.where(line == i, high[:, lanes], packed)
        packed = jnp.where(line == pieces + i, (key_sum - high)[:, lanes], packed)
    sum_at = pieces * head_dim
    sent_state[sum_at : sum_at + 16, :] = packed.astype(BF16)

    pl.semaphore_wait(barrier, n - 1)

    @pl.loop(1, n // 2)
    def _(k):
        state_copy(k).start()

    own_pass.start()
    all_state[me] = sent_state[...]

    @pl.loop(0, chunks)
    def _(to):
        place = lax.broadcasted_iota(jnp.int32, (CHUNK, count), 0) + to * CHUNK
        pick = jnp.where(order_ref[...] == place, 1.0, 0.0).astype(BF16)
        moved = jnp.dot(pick, tokens_ref[...], preferred_element_type=F32)
        sent_tokens[pl.ds(to * frames_per, frames_per)] = moved.reshape(
            frames_per, row_tokens, width
        ).astype(BF16)

    for first in (far, near):

        @pl.loop(0, n // 2)
        def _(k):
            t = first * frames_per + lax.rem(me + k, n // 2)

            @pl.when(t != me)
            def _():
                tok_copy(t).start()

    tile_tokens[me] = sent_tokens[me]

    @pl.loop(1, n // 2)
    def _(k):
        state_copy(k).wait_recv()
        state_pass(k).start()

    @pl.loop(0, n // 2)
    def _(k):
        state_pass(k).wait_recv()

    running[...] = jnp.zeros_like(running)
    prefix[...] = jnp.zeros_like(prefix)

    @pl.loop(0, n)
    def _(f):
        new_group = group_ref[f] != group_ref[jnp.maximum(f - 1, 0)]
        before = jnp.where(new_group, running[...], prefix[...])
        prefix[...] = before
        own = all_state[f].astype(F32)
        running[...] += own
        all_total[f] = before + own

    valid_rows = valid_ref[me] * row_tokens
    loads[2].wait()

    def widen(even, odd):
        column = lax.rem(lax.broadcasted_iota(jnp.int32, even.shape, 0), row_tokens)
        odd_left = jnp.where(column == 0, 0.0, pltpu.roll(odd, 1, 0))
        even_right = jnp.where(column == row_tokens - 1, 0.0, pltpu.roll(even, CHUNK - 1, 0))
        return [x.astype(BF16) for x in (odd_left, even, odd, even_right)]

    def down_copy(c):
        rows = pl.ds(pl.multiple_of(c * CHUNK, CHUNK), CHUNK)
        return pltpu.make_async_remote_copy(
            src_ref=cells.at[1, rows, channels : 3 * channels],
            dst_ref=halo.at[0, rows, :],
            send_sem=halo_send.at[0, c],
            recv_sem=halo_recv.at[0, c],
            device_id={"tm": lax.rem(me + 1, n)},
            device_id_type=MESH,
        )

    def up_copy(c):
        rows = pl.ds(pl.multiple_of(c * CHUNK, CHUNK), CHUNK)
        return pltpu.make_async_remote_copy(
            src_ref=cells.at[0, rows, channels : 3 * channels],
            dst_ref=halo.at[1, rows, :],
            send_sem=halo_send.at[1, c],
            recv_sem=halo_recv.at[1, c],
            device_id={"tm": lax.rem(me + n - 1, n)},
            device_id_type=MESH,
        )

    head_ones = same_head.astype(F32).astype(BF16)
    reach = 3 * channels
    loads[3].wait()

    def advance(c):
        rows = pl.ds(pl.multiple_of(c * CHUNK, CHUNK), CHUNK)

        @pl.loop(0, frames_per)
        def _(k):
            t = c * frames_per + k

            @pl.when(t != me)
            def _():
                tok_arrival(t).wait_recv()

        mixed = jnp.dot(
            flat(tile_tokens[pl.ds(c * frames_per, frames_per)]),
            qkv_ref[:, 0:width],
            preferred_element_type=F32,
        ).astype(BF16)
        rows_ref[...] = jnp.maximum(mixed, jnp.zeros((), BF16)).astype(F32)

        def attend(k, carry):
            f = c * frames_per + k
            total = all_total[f]
            key_total = jnp.concatenate(
                [
                    total[sum_at + i : sum_at + i + 1, :]
                    + total[sum_at + pieces + i : sum_at + pieces + i + 1, :]
                    for i in range(pieces)
                ],
                axis=1,
            )
            here = pl.ds(pl.multiple_of(k * row_tokens, 8), row_tokens)
            query = rows_ref[here, :]
            scaled = (query * key_total).astype(BF16)
            query = query.astype(BF16)
            for b in range(blocks):
                lanes = slice(b * BLOCK, (b + 1) * BLOCK)
                first = b * (BLOCK // 128)
                state = jnp.concatenate(
                    [
                        total[i * head_dim : (i + 1) * head_dim, :]
                        for i in range(first, first + BLOCK // 128)
                    ],
                    axis=1,
                )
                high = state.astype(BF16).astype(F32)
                numer = jnp.zeros((row_tokens, BLOCK), F32)
                for part in (high, state - high):
                    spread = jnp.concatenate([part] * heads_per, axis=0)
                    spread = jnp.where(same_head, spread, 0.0).astype(BF16)
                    numer += jnp.dot(query[:, lanes], spread, preferred_element_type=F32)
                denom = jnp.dot(scaled[:, lanes], head_ones, preferred_element_type=F32) + 1.0
                rows_ref[here, lanes] = numer / denom
            return carry

        lax.fori_loop(0, frames_per, attend, 0, unroll=frames_per <= 4)
        mapped = jnp.dot(rows_ref[...].astype(BF16), outw_ref[...], preferred_element_type=F32)
        row = lax.broadcasted_iota(jnp.int32, mapped.shape, 0) + c * CHUNK
        mapped = jnp.where(row < valid_rows, mapped, 0.0)
        for a in range(2):
            even = mapped[:, 2 * a * channels : (2 * a + 1) * channels]
            odd = mapped[:, (2 * a + 1) * channels : (2 * a + 2) * channels]
            for i, part in enumerate(widen(even, odd)):
                cells[a, rows, i * channels : (i + 1) * channels] = part

        @pl.when(me < n - 1)
        def _():
            down_copy(c).start()

        @pl.when(me > 0)
        def _():
            up_copy(c).start()

        for r in range(2):
            for b in range(2):
                lanes = slice(b * channels, b * channels + reach)
                conv_acc[r, rows, b * channels : (b + 1) * channels] = jnp.dot(
                    cells[0, rows, lanes], convw_ref[1 - r], preferred_element_type=F32
                ) + jnp.dot(cells[1, rows, lanes], convw_ref[2 - r], preferred_element_type=F32)

    @pl.loop(0, half)
    def _(k):
        advance(near + k)

    @pl.loop(0, half)
    def _(k):
        advance(far + k)

    @pl.when(me == 0)
    def _():
        halo[0] = jnp.zeros(halo.shape[1:], BF16)

    @pl.when(me == n - 1)
    def _():
        halo[1] = jnp.zeros(halo.shape[1:], BF16)

    def store(f, r, h):
        pixels = pl.ds(pl.multiple_of(f * 2 * row_tokens, 8), 2 * row_tokens)
        return pltpu.make_async_copy(
            out_buf.at[r, h, pixels, :],
            conv_out.at[f, r, :, h * 128 : (h + 1) * 128],
            store_sem.at[f, r, h],
        )

    sides = [(r, h) for r in range(2) for h in range(channels // 128)]

    stat_acc[...] = jnp.zeros_like(stat_acc)

    @pl.loop(0, chunks)
    def _(c):
        rows = pl.ds(pl.multiple_of(c * CHUNK, CHUNK), CHUNK)

        @pl.when(me > 0)
        def _():
            down_copy(c).wait_recv()

        @pl.when(me < n - 1)
        def _():
            up_copy(c).wait_recv()

        row = lax.broadcasted_iota(jnp.int32, (CHUNK, channels), 0) + c * CHUNK
        for r in range(2):
            edge = halo[r, rows, :].astype(F32)
            parts = widen(edge[:, :channels], edge[:, channels:])
            for b in range(2):
                taps = jnp.concatenate(parts[b : b + 3], axis=1)
                lanes = slice(b * channels, (b + 1) * channels)
                result = conv_acc[r, rows, lanes] + jnp.dot(
                    taps, convw_ref[2 * r], preferred_element_type=F32
                )
                result = jnp.where(row < valid_rows, result, 0.0)
                for h in range(0, channels, 128):
                    out_buf[r, h // 128, pl.ds(c * 2 * CHUNK + b, CHUNK, 2), :] = result[
                        :, h : h + 128
                    ]
                stat_acc[0] += result.reshape(CHUNK // 8, 8, channels).sum(axis=0)

    @pl.loop(0, n)
    def _(f):
        for r, h in sides:
            store(f, r, h).start()

    unit = (4 * row_tokens * group_size)
    group_row = lax.broadcasted_iota(jnp.int32, (channels, channels), 0) // group_size
    group_col = lax.broadcasted_iota(jnp.int32, (channels, channels), 1) // group_size
    group_ones = (group_row == group_col).astype(F32)

    def group_total(part):
        sums = jnp.sum(part, axis=0, keepdims=True)
        return jnp.dot(
            jnp.broadcast_to(sums, (8, channels)),
            group_ones,
            precision=lax.Precision.HIGHEST,
            preferred_element_type=F32,
        )

    tile_sum = group_total(stat_acc[0])
    tile_mean = tile_sum[0:1, :] / (valid_ref[me] * unit).astype(F32)

    @pl.loop(0, 2 * chunks)
    def _(c):
        pixels = pl.ds(pl.multiple_of(c * CHUNK, CHUNK), CHUNK)
        row = lax.broadcasted_iota(jnp.int32, (CHUNK, 128), 0) + c * CHUNK
        for r, h in sides:
            lanes = slice(h * 128, (h + 1) * 128)
            off = jnp.where(row < 2 * valid_rows, out_buf[r, h, pixels, :] - tile_mean[:, lanes], 0.0)
            stat_acc[1, :, lanes] += (off * off).reshape(CHUNK // 8, 8, 128).sum(axis=0)

    tile_square = group_total(stat_acc[1])
    line = lax.broadcasted_iota(jnp.int32, (8, channels), 0)
    sent_stat[...] = jnp.where(line == 0, tile_sum, tile_square)

    @pl.loop(1, n)
    def _(s):
        stat_copy(s).start()

    all_stat[me] = sent_stat[...]

    @pl.loop(1, n)
    def _(s):
        stat_copy(s).wait_recv()

    def add_sum(t, carry):
        total, units = carry
        return total + all_stat[t, 0:1, :], units + valid_ref[t]

    total, units = lax.fori_loop(
        0, n, add_sum, (jnp.zeros((1, channels), F32), jnp.zeros((), jnp.int32))
    )
    total_count = units.astype(F32) * unit
    mean = total / total_count

    def add_square(t, square):
        size = (valid_ref[t] * unit).astype(F32)
        off = all_stat[t, 0:1, :] / size - mean
        return square + all_stat[t, 1:2, :] + size * (off * off)

    square = lax.fori_loop(0, n, add_square, jnp.zeros((1, channels), F32))
    scale = gain_ref[...] * lax.rsqrt(square / total_count + 1e-05)
    norm_ref[...] = jnp.where(
        line == 0, mean, jnp.where(line == 1, scale, valid_ref[me].astype(F32))
    )

    @pl.loop(0, n)
    def _(f):
        for r, h in sides:
            store(f, r, h).wait()

    @pl.loop(0, chunks)
    def _(c):
        @pl.when(me < n - 1)
        def _():
            down_copy(c).wait_send()

        @pl.when(me > 0)
        def _():
            up_copy(c).wait_send()

    @pl.loop(1, n)
    def _(s):
        tok_copy(lax.rem(me + s, n)).wait_send()
        stat_copy(s).wait_send()

    own_pass.wait_send()

    @pl.loop(1, n // 2)
    def _(k):
        state_copy(k).wait_send()
        state_pass(k).wait_send()


def local(
    tokens,
    qkv_weight,
    out_weight,
    conv_weight,
    norm_gain,
    norm_bias,
    group_map,
    token_order,
    valid_frames,
):
    n = lax.axis_size("tm")
    count, width = tokens.shape
    channels = conv_weight.shape[3]
    row_tokens = count // n
    chunks = count // CHUNK
    state_shape = (width // 128 * (width // HEADS) + 16, 128)
    anywhere = pl.BlockSpec(memory_space=pl.ANY)
    vmem = pl.BlockSpec(memory_space=pltpu.VMEM)
    smem = pl.BlockSpec(memory_space=pltpu.SMEM)
    dma = pltpu.SemaphoreType.DMA
    conv, norm = pl.pallas_call(
        functools.partial(mega, n),
        out_shape=(
            jax.ShapeDtypeStruct((n, 2, 2 * row_tokens, channels), F32),
            jax.ShapeDtypeStruct((8, channels), F32),
        ),
        in_specs=[anywhere] * 4 + [vmem, smem, vmem, smem],
        out_specs=(anywhere, vmem),
        scratch_shapes=[
            pltpu.VMEM((count, width), BF16),
            pltpu.VMEM((width, 3 * width), BF16),
            pltpu.VMEM((width, 4 * channels), BF16),
            pltpu.VMEM((3, 3 * channels, channels), BF16),
            pltpu.VMEM((n, row_tokens, width), BF16),
            pltpu.VMEM((n, row_tokens, width), BF16),
            pltpu.VMEM((width // BLOCK, BLOCK, BLOCK), F32),
            pltpu.VMEM((8, width), F32),
            pltpu.VMEM(state_shape, BF16),
            pltpu.VMEM((n,) + state_shape, BF16),
            pltpu.VMEM((n,) + state_shape, F32),
            pltpu.VMEM(state_shape, F32),
            pltpu.VMEM(state_shape, F32),
            pltpu.VMEM((CHUNK, width), F32),
            pltpu.VMEM((2, count, 4 * channels), BF16),
            pltpu.VMEM((2, count, 2 * channels), BF16),
            pltpu.VMEM((2, count, 2 * channels), F32),
            pltpu.VMEM((2, 8, channels), F32),
            pltpu.VMEM((8, channels), F32),
            pltpu.VMEM((n, 8, channels), F32),
            pltpu.VMEM((2, channels // 128, 2 * count, 128), F32),
            dma((4,)),
            dma((n,)),
            dma((n,)),
            dma((n // 2,)),
            dma((n // 2,)),
            dma((n // 2,)),
            dma((n // 2,)),
            dma((2, chunks)),
            dma((2, chunks)),
            dma((n,)),
            dma((n,)),
            dma((n, 2, channels // 128)),
        ],
        compiler_params=pltpu.CompilerParams(
            collective_id=0, has_side_effects=True, vmem_limit_bytes=60 * 1024 * 1024
        ),
    )(
        tokens,
        qkv_weight,
        out_weight,
        conv_weight.reshape(3, 3 * channels, channels),
        norm_gain[None],
        group_map,
        token_order[None],
        valid_frames,
    )
    frame = lax.broadcasted_iota(jnp.int32, conv.shape, 0).astype(F32)
    normed = (conv - norm[0]) * norm[1] + norm_bias
    return jnp.where(frame < norm[2], jax.nn.silu(normed), 0.0).astype(BF16)


def solution(mesh):
    in_specs = (P(("clip", "tm"), None), P(), P(), P(), P(), P(), P("clip"), P("clip"), P("clip"))
    out_specs = P("clip", "tm", None, None)
    return jax.shard_map(local, mesh=mesh, in_specs=in_specs, out_specs=out_specs, check_vma=False)
```

```python
import functools

import jax
import jax.numpy as jnp
from jax import lax
from jax.experimental import pallas as pl
from jax.experimental.pallas import tpu as pltpu
from jax.sharding import PartitionSpec as P

HEADS = 16
NORM_GROUPS = 32
MESH = pl.DeviceIdType.MESH
F32 = jnp.float32
BF16 = jnp.bfloat16
CHUNK = 256
BLOCK = 256


def flat(cells):
    frames, rows, width = cells.shape
    if rows % 16 == 0:
        return cells.reshape(frames * rows, width)
    return cells.astype(F32).reshape(frames * rows, width).astype(BF16)


def mega(
    n,
    tokens_hbm,
    qkv_hbm,
    out_hbm,
    conv_hbm,
    gain_ref,
    group_ref,
    order_ref,
    valid_ref,
    conv_out,
    norm_ref,
    tokens_ref,
    qkv_ref,
    outw_ref,
    convw_ref,
    sent_tokens,
    tile_tokens,
    state_acc,
    sum_acc,
    sent_state,
    all_state,
    all_total,
    running,
    prefix,
    rows_ref,
    cells,
    halo,
    conv_acc,
    stat_acc,
    sent_stat,
    all_stat,
    out_buf,
    load_sem,
    tok_send,
    tok_recv,
    st_send,
    st_recv,
    pass_send,
    pass_recv,
    halo_send,
    halo_recv,
    stat_send,
    stat_recv,
    store_sem,
):
    me = lax.axis_index("tm")
    count, width = tokens_ref.shape
    row_tokens = count // n
    chunks = count // CHUNK
    frames_per = CHUNK // row_tokens
    head_dim = width // HEADS
    channels = gain_ref.shape[1]
    blocks = width // BLOCK
    heads_per = BLOCK // head_dim
    group_size = channels // NORM_GROUPS

    loads = [
        pltpu.make_async_copy(a, b, load_sem.at[i])
        for i, (a, b) in enumerate(
            [
                (tokens_hbm, tokens_ref),
                (qkv_hbm, qkv_ref),
                (out_hbm, outw_ref),
                (conv_hbm, convw_ref),
            ]
        )
    ]
    for load in loads:
        load.start()

    barrier = pltpu.get_barrier_semaphore()

    @pl.loop(1, n)
    def _(s):
        pl.semaphore_signal(
            barrier, inc=1, device_id={"tm": lax.rem(me + s, n)}, device_id_type=MESH
        )

    def exchange(s, src, dst, send_sem, recv_sem):
        return pltpu.make_async_remote_copy(
            src_ref=src,
            dst_ref=dst,
            send_sem=send_sem.at[s],
            recv_sem=recv_sem.at[s],
            device_id={"tm": lax.rem(me + s, n)},
            device_id_type=MESH,
        )

    def tok_copy(t):
        return pltpu.make_async_remote_copy(
            src_ref=sent_tokens.at[t],
            dst_ref=tile_tokens.at[me],
            send_sem=tok_send.at[t],
            recv_sem=tok_recv.at[me],
            device_id={"tm": t},
            device_id_type=MESH,
        )

    def tok_arrival(t):
        return pltpu.make_async_remote_copy(
            src_ref=sent_tokens.at[t],
            dst_ref=tile_tokens.at[t],
            send_sem=tok_send.at[t],
            recv_sem=tok_recv.at[t],
            device_id={"tm": t},
            device_id_type=MESH,
        )

    partner = me + 1 - 2 * lax.rem(me, 2)

    def state_copy(k):
        return pltpu.make_async_remote_copy(
            src_ref=sent_state,
            dst_ref=all_state.at[me],
            send_sem=st_send.at[k],
            recv_sem=st_recv.at[k],
            device_id={"tm": lax.rem(me + 2 * k, n)},
            device_id_type=MESH,
        )

    def state_pass(k):
        source = lax.rem(me + n - 2 * k, n)
        return pltpu.make_async_remote_copy(
            src_ref=all_state.at[source],
            dst_ref=all_state.at[source],
            send_sem=pass_send.at[k],
            recv_sem=pass_recv.at[k],
            device_id={"tm": partner},
            device_id_type=MESH,
        )

    own_pass = pltpu.make_async_remote_copy(
        src_ref=sent_state,
        dst_ref=all_state.at[me],
        send_sem=pass_send.at[0],
        recv_sem=pass_recv.at[0],
        device_id={"tm": partner},
        device_id_type=MESH,
    )

    def stat_copy(s):
        return exchange(s, sent_stat, all_stat.at[me], stat_send, stat_recv)

    half = chunks // 2
    near = lax.div(me, n // 2) * half
    far = half - near

    loads[0].wait()

    @pl.loop(0, chunks)
    def _(to):
        place = lax.broadcasted_iota(jnp.int32, (CHUNK, count), 0) + to * CHUNK
        pick = jnp.where(order_ref[...] == place, 1.0, 0.0).astype(BF16)
        moved = jnp.dot(pick, tokens_ref[...], preferred_element_type=F32)
        sent_tokens[pl.ds(to * frames_per, frames_per)] = moved.reshape(
            frames_per, row_tokens, width
        ).astype(BF16)

    pl.semaphore_wait(barrier, n - 1)

    def send_tokens(first, start, stop):
        @pl.loop(start, stop)
        def _(k):
            t = first * frames_per + lax.rem(me + k, n // 2)

            @pl.when(t != me)
            def _():
                tok_copy(t).start()

    send_tokens(far, 0, n // 4)
    tile_tokens[me] = sent_tokens[me]

    loads[1].wait()
    state_acc[...] = jnp.zeros_like(state_acc)
    sum_acc[...] = jnp.zeros_like(sum_acc)

    @pl.loop(0, chunks)
    def _(c):
        rows = pl.ds(pl.multiple_of(c * CHUNK, CHUNK), CHUNK)
        mixed = jnp.dot(
            tokens_ref[rows, :], qkv_ref[:, width : 3 * width], preferred_element_type=F32
        ).astype(BF16)
        keys = jnp.maximum(mixed[:, :width], jnp.zeros((), BF16))
        sum_acc[...] += keys.astype(F32).reshape(CHUNK // 8, 8, width).sum(axis=0)
        for b in range(blocks):
            lanes = slice(b * BLOCK, (b + 1) * BLOCK)
            state_acc[b] += lax.dot_general(
                keys[:, lanes],
                mixed[:, width + b * BLOCK : width + (b + 1) * BLOCK],
                (((0,), (0,)), ((), ())),
                preferred_element_type=F32,
            )

    head_row = lax.broadcasted_iota(jnp.int32, (BLOCK, BLOCK), 0) // head_dim
    head_col = lax.broadcasted_iota(jnp.int32, (BLOCK, BLOCK), 1) // head_dim
    same_head = head_row == head_col
    pieces = width // 128
    for b in range(blocks):
        own = jnp.where(same_head, state_acc[b], 0.0)
        own = own.reshape(heads_per, head_dim, BLOCK).sum(axis=0).astype(BF16)
        for i in range(BLOCK // 128):
            at = (b * (BLOCK // 128) + i) * head_dim
            sent_state[at : at + head_dim, :] = own[:, i * 128 : (i + 1) * 128]
    key_sum = jnp.sum(sum_acc[...], axis=0, keepdims=True)
    high = key_sum.astype(BF16).astype(F32)
    line = lax.broadcasted_iota(jnp.int32, (16, 128), 0)
    packed = jnp.zeros((16, 128), F32)
    for i in range(pieces):
        lanes = slice(i * 128, (i + 1) * 128)
        packed = jnp.where(line == i, high[:, lanes], packed)
        packed = jnp.where(line == pieces + i, (key_sum - high)[:, lanes], packed)
    sum_at = pieces * head_dim
    sent_state[sum_at : sum_at + 16, :] = packed.astype(BF16)

    @pl.loop(1, n // 2)
    def _(k):
        state_copy(k).start()

    own_pass.start()
    all_state[me] = sent_state[...]

    send_tokens(near, 0, n // 2)
    send_tokens(far, n // 4, n // 2)

    @pl.loop(1, n // 2)
    def _(k):
        state_copy(k).wait_recv()
        state_pass(k).start()

    @pl.loop(0, n // 2)
    def _(k):
        state_pass(k).wait_recv()

    running[...] = jnp.zeros_like(running)
    prefix[...] = jnp.zeros_like(prefix)

    @pl.loop(0, n)
    def _(f):
        new_group = group_ref[f] != group_ref[jnp.maximum(f - 1, 0)]
        before = jnp.where(new_group, running[...], prefix[...])
        prefix[...] = before
        own = all_state[f].astype(F32)
        running[...] += own
        all_total[f] = before + own

    valid_rows = valid_ref[me] * row_tokens
    loads[2].wait()

    def widen(even, odd):
        column = lax.rem(lax.broadcasted_iota(jnp.int32, even.shape, 0), row_tokens)
        odd_left = jnp.where(column == 0, 0.0, pltpu.roll(odd, 1, 0))
        even_right = jnp.where(column == row_tokens - 1, 0.0, pltpu.roll(even, CHUNK - 1, 0))
        return [x.astype(BF16) for x in (odd_left, even, odd, even_right)]

    def down_copy(c):
        rows = pl.ds(pl.multiple_of(c * CHUNK, CHUNK), CHUNK)
        return pltpu.make_async_remote_copy(
            src_ref=cells.at[1, rows, channels : 3 * channels],
            dst_ref=halo.at[0, rows, :],
            send_sem=halo_send.at[0, c],
            recv_sem=halo_recv.at[0, c],
            device_id={"tm": lax.rem(me + 1, n)},
            device_id_type=MESH,
        )

    def up_copy(c):
        rows = pl.ds(pl.multiple_of(c * CHUNK, CHUNK), CHUNK)
        return pltpu.make_async_remote_copy(
            src_ref=cells.at[0, rows, channels : 3 * channels],
            dst_ref=halo.at[1, rows, :],
            send_sem=halo_send.at[1, c],
            recv_sem=halo_recv.at[1, c],
            device_id={"tm": lax.rem(me + n - 1, n)},
            device_id_type=MESH,
        )

    head_ones = same_head.astype(F32).astype(BF16)
    reach = 3 * channels
    loads[3].wait()

    def advance(c):
        rows = pl.ds(pl.multiple_of(c * CHUNK, CHUNK), CHUNK)

        @pl.loop(0, frames_per)
        def _(k):
            t = c * frames_per + k

            @pl.when(t != me)
            def _():
                tok_arrival(t).wait_recv()

        mixed = jnp.dot(
            flat(tile_tokens[pl.ds(c * frames_per, frames_per)]),
            qkv_ref[:, 0:width],
            preferred_element_type=F32,
        ).astype(BF16)
        rows_ref[...] = jnp.maximum(mixed, jnp.zeros((), BF16)).astype(F32)

        def attend(k, carry):
            f = c * frames_per + k
            total = all_total[f]
            key_total = jnp.concatenate(
                [
                    total[sum_at + i : sum_at + i + 1, :]
                    + total[sum_at + pieces + i : sum_at + pieces + i + 1, :]
                    for i in range(pieces)
                ],
                axis=1,
            )
            here = pl.ds(pl.multiple_of(k * row_tokens, 8), row_tokens)
            query = rows_ref[here, :]
            scaled = (query * key_total).astype(BF16)
            query = query.astype(BF16)
            for b in range(blocks):
                lanes = slice(b * BLOCK, (b + 1) * BLOCK)
                first = b * (BLOCK // 128)
                state = jnp.concatenate(
                    [
                        total[i * head_dim : (i + 1) * head_dim, :]
                        for i in range(first, first + BLOCK // 128)
                    ],
                    axis=1,
                )
                high = state.astype(BF16).astype(F32)
                numer = jnp.zeros((row_tokens, BLOCK), F32)
                for part in (high, state - high):
                    spread = jnp.concatenate([part] * heads_per, axis=0)
                    spread = jnp.where(same_head, spread, 0.0).astype(BF16)
                    numer += jnp.dot(query[:, lanes], spread, preferred_element_type=F32)
                denom = jnp.dot(scaled[:, lanes], head_ones, preferred_element_type=F32) + 1.0
                rows_ref[here, lanes] = numer / denom
            return carry

        lax.fori_loop(0, frames_per, attend, 0, unroll=frames_per <= 4)
        mapped = jnp.dot(rows_ref[...].astype(BF16), outw_ref[...], preferred_element_type=F32)
        row = lax.broadcasted_iota(jnp.int32, mapped.shape, 0) + c * CHUNK
        mapped = jnp.where(row < valid_rows, mapped, 0.0)
        for a in range(2):
            even = mapped[:, 2 * a * channels : (2 * a + 1) * channels]
            odd = mapped[:, (2 * a + 1) * channels : (2 * a + 2) * channels]
            for i, part in enumerate(widen(even, odd)):
                cells[a, rows, i * channels : (i + 1) * channels] = part

        @pl.when(me < n - 1)
        def _():
            down_copy(c).start()

        @pl.when(me > 0)
        def _():
            up_copy(c).start()

    def convolve(c):
        rows = pl.ds(pl.multiple_of(c * CHUNK, CHUNK), CHUNK)
        for r in range(2):
            for b in range(2):
                lanes = slice(b * channels, b * channels + reach)
                conv_acc[r, rows, b * channels : (b + 1) * channels] = jnp.dot(
                    cells[0, rows, lanes], convw_ref[1 - r], preferred_element_type=F32
                ) + jnp.dot(cells[1, rows, lanes], convw_ref[2 - r], preferred_element_type=F32)

    @pl.loop(0, half)
    def _(k):
        advance(near + k)
        convolve(near + k)

    @pl.loop(0, half)
    def _(k):
        advance(far + k)

    @pl.loop(0, half)
    def _(k):
        convolve(far + k)

    @pl.when(me == 0)
    def _():
        halo[0] = jnp.zeros(halo.shape[1:], BF16)

    @pl.when(me == n - 1)
    def _():
        halo[1] = jnp.zeros(halo.shape[1:], BF16)

    def store(f, r, h):
        pixels = pl.ds(pl.multiple_of(f * 2 * row_tokens, 8), 2 * row_tokens)
        return pltpu.make_async_copy(
            out_buf.at[r, h, pixels, :],
            conv_out.at[f, r, :, h * 128 : (h + 1) * 128],
            store_sem.at[f, r, h],
        )

    sides = [(r, h) for r in range(2) for h in range(channels // 128)]

    stat_acc[...] = jnp.zeros_like(stat_acc)

    @pl.loop(0, chunks)
    def _(c):
        rows = pl.ds(pl.multiple_of(c * CHUNK, CHUNK), CHUNK)

        @pl.when(me > 0)
        def _():
            down_copy(c).wait_recv()

        @pl.when(me < n - 1)
        def _():
            up_copy(c).wait_recv()

        row = lax.broadcasted_iota(jnp.int32, (CHUNK, channels), 0) + c * CHUNK
        for r in range(2):
            edge = halo[r, rows, :].astype(F32)
            parts = widen(edge[:, :channels], edge[:, channels:])
            for b in range(2):
                taps = jnp.concatenate(parts[b : b + 3], axis=1)
                lanes = slice(b * channels, (b + 1) * channels)
                result = conv_acc[r, rows, lanes] + jnp.dot(
                    taps, convw_ref[2 * r], preferred_element_type=F32
                )
                result = jnp.where(row < valid_rows, result, 0.0)
                for h in range(0, channels, 128):
                    out_buf[r, h // 128, pl.ds(c * 2 * CHUNK + b, CHUNK, 2), :] = result[
                        :, h : h + 128
                    ]
                stat_acc[0] += result.reshape(CHUNK // 8, 8, channels).sum(axis=0)

    @pl.loop(0, n)
    def _(f):
        for r, h in sides:
            store(f, r, h).start()

    unit = (4 * row_tokens * group_size)
    group_row = lax.broadcasted_iota(jnp.int32, (channels, channels), 0) // group_size
    group_col = lax.broadcasted_iota(jnp.int32, (channels, channels), 1) // group_size
    group_ones = (group_row == group_col).astype(F32)

    def group_total(part):
        sums = jnp.sum(part, axis=0, keepdims=True)
        return jnp.dot(
            jnp.broadcast_to(sums, (8, channels)),
            group_ones,
            precision=lax.Precision.HIGHEST,
            preferred_element_type=F32,
        )

    tile_sum = group_total(stat_acc[0])
    tile_mean = tile_sum[0:1, :] / (valid_ref[me] * unit).astype(F32)

    @pl.loop(0, 2 * chunks)
    def _(c):
        pixels = pl.ds(pl.multiple_of(c * CHUNK, CHUNK), CHUNK)
        row = lax.broadcasted_iota(jnp.int32, (CHUNK, 128), 0) + c * CHUNK
        for r, h in sides:
            lanes = slice(h * 128, (h + 1) * 128)
            off = jnp.where(row < 2 * valid_rows, out_buf[r, h, pixels, :] - tile_mean[:, lanes], 0.0)
            stat_acc[1, :, lanes] += (off * off).reshape(CHUNK // 8, 8, 128).sum(axis=0)

    tile_square = group_total(stat_acc[1])
    line = lax.broadcasted_iota(jnp.int32, (8, channels), 0)
    sent_stat[...] = jnp.where(line == 0, tile_sum, tile_square)

    @pl.loop(1, n)
    def _(s):
        stat_copy(s).start()

    all_stat[me] = sent_stat[...]

    @pl.loop(1, n)
    def _(s):
        stat_copy(s).wait_recv()

    def add_sum(t, carry):
        total, units = carry
        return total + all_stat[t, 0:1, :], units + valid_ref[t]

    total, units = lax.fori_loop(
        0, n, add_sum, (jnp.zeros((1, channels), F32), jnp.zeros((), jnp.int32))
    )
    total_count = units.astype(F32) * unit
    mean = total / total_count

    def add_square(t, square):
        size = (valid_ref[t] * unit).astype(F32)
        off = all_stat[t, 0:1, :] / size - mean
        return square + all_stat[t, 1:2, :] + size * (off * off)

    square = lax.fori_loop(0, n, add_square, jnp.zeros((1, channels), F32))
    scale = gain_ref[...] * lax.rsqrt(square / total_count + 1e-05)
    norm_ref[...] = jnp.where(
        line == 0, mean, jnp.where(line == 1, scale, valid_ref[me].astype(F32))
    )

    @pl.loop(0, n)
    def _(f):
        for r, h in sides:
            store(f, r, h).wait()

    @pl.loop(0, chunks)
    def _(c):
        @pl.when(me < n - 1)
        def _():
            down_copy(c).wait_send()

        @pl.when(me > 0)
        def _():
            up_copy(c).wait_send()

    @pl.loop(1, n)
    def _(s):
        tok_copy(lax.rem(me + s, n)).wait_send()
        stat_copy(s).wait_send()

    own_pass.wait_send()

    @pl.loop(1, n // 2)
    def _(k):
        state_copy(k).wait_send()
        state_pass(k).wait_send()


def local(
    tokens,
    qkv_weight,
    out_weight,
    conv_weight,
    norm_gain,
    norm_bias,
    group_map,
    token_order,
    valid_frames,
):
    n = lax.axis_size("tm")
    count, width = tokens.shape
    channels = conv_weight.shape[3]
    row_tokens = count // n
    chunks = count // CHUNK
    state_shape = (width // 128 * (width // HEADS) + 16, 128)
    anywhere = pl.BlockSpec(memory_space=pl.ANY)
    vmem = pl.BlockSpec(memory_space=pltpu.VMEM)
    smem = pl.BlockSpec(memory_space=pltpu.SMEM)
    dma = pltpu.SemaphoreType.DMA
    conv, norm = pl.pallas_call(
        functools.partial(mega, n),
        out_shape=(
            jax.ShapeDtypeStruct((n, 2, 2 * row_tokens, channels), F32),
            jax.ShapeDtypeStruct((8, channels), F32),
        ),
        in_specs=[anywhere] * 4 + [vmem, smem, vmem, smem],
        out_specs=(anywhere, vmem),
        scratch_shapes=[
            pltpu.VMEM((count, width), BF16),
            pltpu.VMEM((width, 3 * width), BF16),
            pltpu.VMEM((width, 4 * channels), BF16),
            pltpu.VMEM((3, 3 * channels, channels), BF16),
            pltpu.VMEM((n, row_tokens, width), BF16),
            pltpu.VMEM((n, row_tokens, width), BF16),
            pltpu.VMEM((width // BLOCK, BLOCK, BLOCK), F32),
            pltpu.VMEM((8, width), F32),
            pltpu.VMEM(state_shape, BF16),
            pltpu.VMEM((n,) + state_shape, BF16),
            pltpu.VMEM((n,) + state_shape, F32),
            pltpu.VMEM(state_shape, F32),
            pltpu.VMEM(state_shape, F32),
            pltpu.VMEM((CHUNK, width), F32),
            pltpu.VMEM((2, count, 4 * channels), BF16),
            pltpu.VMEM((2, count, 2 * channels), BF16),
            pltpu.VMEM((2, count, 2 * channels), F32),
            pltpu.VMEM((2, 8, channels), F32),
            pltpu.VMEM((8, channels), F32),
            pltpu.VMEM((n, 8, channels), F32),
            pltpu.VMEM((2, channels // 128, 2 * count, 128), F32),
            dma((4,)),
            dma((n,)),
            dma((n,)),
            dma((n // 2,)),
            dma((n // 2,)),
            dma((n // 2,)),
            dma((n // 2,)),
            dma((2, chunks)),
            dma((2, chunks)),
            dma((n,)),
            dma((n,)),
            dma((n, 2, channels // 128)),
        ],
        compiler_params=pltpu.CompilerParams(
            collective_id=0, has_side_effects=True, vmem_limit_bytes=60 * 1024 * 1024
        ),
    )(
        tokens,
        qkv_weight,
        out_weight,
        conv_weight.reshape(3, 3 * channels, channels),
        norm_gain[None],
        group_map,
        token_order[None],
        valid_frames,
    )
    frame = lax.broadcasted_iota(jnp.int32, conv.shape, 0).astype(F32)
    normed = (conv - norm[0]) * norm[1] + norm_bias
    return jnp.where(frame < norm[2], jax.nn.silu(normed), 0.0).astype(BF16)


def solution(mesh):
    in_specs = (P(("clip", "tm"), None), P(), P(), P(), P(), P(), P("clip"), P("clip"), P("clip"))
    out_specs = P("clip", "tm", None, None)
    return jax.shard_map(local, mesh=mesh, in_specs=in_specs, out_specs=out_specs, check_vma=False)
```

```python
import functools

import jax
import jax.numpy as jnp
from jax import lax
from jax.experimental import pallas as pl
from jax.experimental.pallas import tpu as pltpu
from jax.sharding import PartitionSpec as P

HEADS = 16
NORM_GROUPS = 32
MESH = pl.DeviceIdType.MESH
F32 = jnp.float32
BF16 = jnp.bfloat16
CHUNK = 256
BLOCK = 256


def flat(cells):
    frames, rows, width = cells.shape
    if rows % 16 == 0:
        return cells.reshape(frames * rows, width)
    return cells.astype(F32).reshape(frames * rows, width).astype(BF16)


def mega(
    n,
    tokens_hbm,
    qkv_hbm,
    out_hbm,
    conv_hbm,
    gain_ref,
    group_ref,
    order_ref,
    valid_ref,
    conv_out,
    norm_ref,
    tokens_ref,
    qkv_ref,
    outw_ref,
    convw_ref,
    sent_tokens,
    tile_tokens,
    state_acc,
    sum_acc,
    sent_state,
    all_state,
    all_total,
    running,
    prefix,
    rows_ref,
    cells,
    halo,
    conv_acc,
    stat_acc,
    sent_stat,
    all_stat,
    out_buf,
    load_sem,
    tok_send,
    tok_recv,
    st_send,
    st_recv,
    pass_send,
    pass_recv,
    halo_send,
    halo_recv,
    stat_send,
    stat_recv,
    store_sem,
):
    me = lax.axis_index("tm")
    count, width = tokens_ref.shape
    row_tokens = count // n
    chunks = count // CHUNK
    frames_per = CHUNK // row_tokens
    head_dim = width // HEADS
    channels = gain_ref.shape[1]
    blocks = width // BLOCK
    heads_per = BLOCK // head_dim
    group_size = channels // NORM_GROUPS

    loads = [
        pltpu.make_async_copy(a, b, load_sem.at[i])
        for i, (a, b) in enumerate(
            [
                (tokens_hbm, tokens_ref),
                (qkv_hbm, qkv_ref),
                (out_hbm, outw_ref),
                (conv_hbm, convw_ref),
            ]
        )
    ]
    for load in loads:
        load.start()

    barrier = pltpu.get_barrier_semaphore()

    @pl.loop(1, n)
    def _(s):
        pl.semaphore_signal(
            barrier, inc=1, device_id={"tm": lax.rem(me + s, n)}, device_id_type=MESH
        )

    def exchange(s, src, dst, send_sem, recv_sem):
        return pltpu.make_async_remote_copy(
            src_ref=src,
            dst_ref=dst,
            send_sem=send_sem.at[s],
            recv_sem=recv_sem.at[s],
            device_id={"tm": lax.rem(me + s, n)},
            device_id_type=MESH,
        )

    def tok_copy(t):
        return pltpu.make_async_remote_copy(
            src_ref=sent_tokens.at[t],
            dst_ref=tile_tokens.at[me],
            send_sem=tok_send.at[t],
            recv_sem=tok_recv.at[me],
            device_id={"tm": t},
            device_id_type=MESH,
        )

    def tok_arrival(t):
        return pltpu.make_async_remote_copy(
            src_ref=sent_tokens.at[t],
            dst_ref=tile_tokens.at[t],
            send_sem=tok_send.at[t],
            recv_sem=tok_recv.at[t],
            device_id={"tm": t},
            device_id_type=MESH,
        )

    partner = me + 1 - 2 * lax.rem(me, 2)

    def state_copy(k):
        return pltpu.make_async_remote_copy(
            src_ref=sent_state,
            dst_ref=all_state.at[me],
            send_sem=st_send.at[k],
            recv_sem=st_recv.at[k],
            device_id={"tm": lax.rem(me + 2 * k, n)},
            device_id_type=MESH,
        )

    def state_pass(k):
        source = lax.rem(me + n - 2 * k, n)
        return pltpu.make_async_remote_copy(
            src_ref=all_state.at[source],
            dst_ref=all_state.at[source],
            send_sem=pass_send.at[k],
            recv_sem=pass_recv.at[k],
            device_id={"tm": partner},
            device_id_type=MESH,
        )

    own_pass = pltpu.make_async_remote_copy(
        src_ref=sent_state,
        dst_ref=all_state.at[me],
        send_sem=pass_send.at[0],
        recv_sem=pass_recv.at[0],
        device_id={"tm": partner},
        device_id_type=MESH,
    )

    def stat_copy(s):
        return exchange(s, sent_stat, all_stat.at[me], stat_send, stat_recv)

    half = chunks // 2
    near = lax.div(me, n // 2) * half
    far = half - near

    loads[0].wait()
    loads[1].wait()
    state_acc[...] = jnp.zeros_like(state_acc)
    sum_acc[...] = jnp.zeros_like(sum_acc)

    @pl.loop(0, chunks)
    def _(c):
        rows = pl.ds(pl.multiple_of(c * CHUNK, CHUNK), CHUNK)
        mixed = jnp.dot(
            tokens_ref[rows, :], qkv_ref[:, width : 3 * width], preferred_element_type=F32
        ).astype(BF16)
        keys = jnp.maximum(mixed[:, :width], jnp.zeros((), BF16))
        sum_acc[...] += keys.astype(F32).reshape(CHUNK // 8, 8, width).sum(axis=0)
        for b in range(blocks):
            lanes = slice(b * BLOCK, (b + 1) * BLOCK)
            state_acc[b] += lax.dot_general(
                keys[:, lanes],
                mixed[:, width + b * BLOCK : width + (b + 1) * BLOCK],
                (((0,), (0,)), ((), ())),
                preferred_element_type=F32,
            )

    head_row = lax.broadcasted_iota(jnp.int32, (BLOCK, BLOCK), 0) // head_dim
    head_col = lax.broadcasted_iota(jnp.int32, (BLOCK, BLOCK), 1) // head_dim
    same_head = head_row == head_col
    pieces = width // 128
    for b in range(blocks):
        own = jnp.where(same_head, state_acc[b], 0.0)
        own = own.reshape(heads_per, head_dim, BLOCK).sum(axis=0).astype(BF16)
        for i in range(BLOCK // 128):
            at = (b * (BLOCK // 128) + i) * head_dim
            sent_state[at : at + head_dim, :] = own[:, i * 128 : (i + 1) * 128]
    key_sum = jnp.sum(sum_acc[...], axis=0, keepdims=True)
    high = key_sum.astype(BF16).astype(F32)
    line = lax.broadcasted_iota(jnp.int32, (16, 128), 0)
    packed = jnp.zeros((16, 128), F32)
    for i in range(pieces):
        lanes = slice(i * 128, (i + 1) * 128)
        packed = jnp.where(line == i, high[:, lanes], packed)
        packed = jnp.where(line == pieces + i, (key_sum - high)[:, lanes], packed)
    sum_at = pieces * head_dim
    sent_state[sum_at : sum_at + 16, :] = packed.astype(BF16)

    pl.semaphore_wait(barrier, n - 1)

    @pl.loop(1, n // 2)
    def _(k):
        state_copy(k).start()

    own_pass.start()
    all_state[me] = sent_state[...]

    @pl.loop(0, chunks)
    def _(to):
        place = lax.broadcasted_iota(jnp.int32, (CHUNK, count), 0) + to * CHUNK
        pick = jnp.where(order_ref[...] == place, 1.0, 0.0).astype(BF16)
        moved = jnp.dot(pick, tokens_ref[...], preferred_element_type=F32)
        sent_tokens[pl.ds(to * frames_per, frames_per)] = moved.reshape(
            frames_per, row_tokens, width
        ).astype(BF16)

    for first in (near, far):

        @pl.loop(0, n // 2)
        def _(k):
            t = first * frames_per + lax.rem(me + k, n // 2)

            @pl.when(t != me)
            def _():
                tok_copy(t).start()

    tile_tokens[me] = sent_tokens[me]

    @pl.loop(1, n // 2)
    def _(k):
        state_copy(k).wait_recv()
        state_pass(k).start()

    @pl.loop(0, n // 2)
    def _(k):
        state_pass(k).wait_recv()

    running[...] = jnp.zeros_like(running)
    prefix[...] = jnp.zeros_like(prefix)

    @pl.loop(0, n)
    def _(f):
        new_group = group_ref[f] != group_ref[jnp.maximum(f - 1, 0)]
        before = jnp.where(new_group, running[...], prefix[...])
        prefix[...] = before
        own = all_state[f].astype(F32)
        running[...] += own
        all_total[f] = before + own

    valid_rows = valid_ref[me] * row_tokens
    loads[2].wait()

    def widen(even, odd):
        column = lax.rem(lax.broadcasted_iota(jnp.int32, even.shape, 0), row_tokens)
        odd_left = jnp.where(column == 0, 0.0, pltpu.roll(odd, 1, 0))
        even_right = jnp.where(column == row_tokens - 1, 0.0, pltpu.roll(even, CHUNK - 1, 0))
        return [x.astype(BF16) for x in (odd_left, even, odd, even_right)]

    def down_copy(c):
        rows = pl.ds(pl.multiple_of(c * CHUNK, CHUNK), CHUNK)
        return pltpu.make_async_remote_copy(
            src_ref=cells.at[1, rows, channels : 3 * channels],
            dst_ref=halo.at[0, rows, :],
            send_sem=halo_send.at[0, c],
            recv_sem=halo_recv.at[0, c],
            device_id={"tm": lax.rem(me + 1, n)},
            device_id_type=MESH,
        )

    def up_copy(c):
        rows = pl.ds(pl.multiple_of(c * CHUNK, CHUNK), CHUNK)
        return pltpu.make_async_remote_copy(
            src_ref=cells.at[0, rows, channels : 3 * channels],
            dst_ref=halo.at[1, rows, :],
            send_sem=halo_send.at[1, c],
            recv_sem=halo_recv.at[1, c],
            device_id={"tm": lax.rem(me + n - 1, n)},
            device_id_type=MESH,
        )

    head_ones = same_head.astype(F32).astype(BF16)
    reach = 3 * channels
    loads[3].wait()

    def advance(c):
        rows = pl.ds(pl.multiple_of(c * CHUNK, CHUNK), CHUNK)

        @pl.loop(0, frames_per)
        def _(k):
            t = c * frames_per + k

            @pl.when(t != me)
            def _():
                tok_arrival(t).wait_recv()

        mixed = jnp.dot(
            flat(tile_tokens[pl.ds(c * frames_per, frames_per)]),
            qkv_ref[:, 0:width],
            preferred_element_type=F32,
        ).astype(BF16)
        rows_ref[...] = jnp.maximum(mixed, jnp.zeros((), BF16)).astype(F32)

        def attend(k, carry):
            f = c * frames_per + k
            total = all_total[f]
            key_total = jnp.concatenate(
                [
                    total[sum_at + i : sum_at + i + 1, :]
                    + total[sum_at + pieces + i : sum_at + pieces + i + 1, :]
                    for i in range(pieces)
                ],
                axis=1,
            )
            here = pl.ds(pl.multiple_of(k * row_tokens, 8), row_tokens)
            query = rows_ref[here, :]
            scaled = (query * key_total).astype(BF16)
            query = query.astype(BF16)
            for b in range(blocks):
                lanes = slice(b * BLOCK, (b + 1) * BLOCK)
                first = b * (BLOCK // 128)
                state = jnp.concatenate(
                    [
                        total[i * head_dim : (i + 1) * head_dim, :]
                        for i in range(first, first + BLOCK // 128)
                    ],
                    axis=1,
                )
                high = state.astype(BF16).astype(F32)
                numer = jnp.zeros((row_tokens, BLOCK), F32)
                for part in (high, state - high):
                    spread = jnp.concatenate([part] * heads_per, axis=0)
                    spread = jnp.where(same_head, spread, 0.0).astype(BF16)
                    numer += jnp.dot(query[:, lanes], spread, preferred_element_type=F32)
                denom = jnp.dot(scaled[:, lanes], head_ones, preferred_element_type=F32) + 1.0
                rows_ref[here, lanes] = numer / denom
            return carry

        lax.fori_loop(0, frames_per, attend, 0, unroll=frames_per <= 4)
        mapped = jnp.dot(rows_ref[...].astype(BF16), outw_ref[...], preferred_element_type=F32)
        row = lax.broadcasted_iota(jnp.int32, mapped.shape, 0) + c * CHUNK
        mapped = jnp.where(row < valid_rows, mapped, 0.0)
        for a in range(2):
            even = mapped[:, 2 * a * channels : (2 * a + 1) * channels]
            odd = mapped[:, (2 * a + 1) * channels : (2 * a + 2) * channels]
            for i, part in enumerate(widen(even, odd)):
                cells[a, rows, i * channels : (i + 1) * channels] = part

        @pl.when(me < n - 1)
        def _():
            down_copy(c).start()

        @pl.when(me > 0)
        def _():
            up_copy(c).start()

        for r in range(2):
            for b in range(2):
                lanes = slice(b * channels, b * channels + reach)
                conv_acc[r, rows, b * channels : (b + 1) * channels] = jnp.dot(
                    cells[0, rows, lanes], convw_ref[1 - r], preferred_element_type=F32
                ) + jnp.dot(cells[1, rows, lanes], convw_ref[2 - r], preferred_element_type=F32)

    @pl.loop(0, half)
    def _(k):
        advance(near + k)

    @pl.loop(0, half)
    def _(k):
        advance(far + k)

    @pl.when(me == 0)
    def _():
        halo[0] = jnp.zeros(halo.shape[1:], BF16)

    @pl.when(me == n - 1)
    def _():
        halo[1] = jnp.zeros(halo.shape[1:], BF16)

    def store(f, r, h):
        pixels = pl.ds(pl.multiple_of(f * 2 * row_tokens, 8), 2 * row_tokens)
        return pltpu.make_async_copy(
            out_buf.at[r, h, pixels, :],
            conv_out.at[f, r, :, h * 128 : (h + 1) * 128],
            store_sem.at[f, r, h],
        )

    sides = [(r, h) for r in range(2) for h in range(channels // 128)]

    stat_acc[...] = jnp.zeros_like(stat_acc)

    @pl.loop(0, chunks)
    def _(c):
        rows = pl.ds(pl.multiple_of(c * CHUNK, CHUNK), CHUNK)

        @pl.when(me > 0)
        def _():
            down_copy(c).wait_recv()

        @pl.when(me < n - 1)
        def _():
            up_copy(c).wait_recv()

        row = lax.broadcasted_iota(jnp.int32, (CHUNK, channels), 0) + c * CHUNK
        for r in range(2):
            edge = halo[r, rows, :].astype(F32)
            parts = widen(edge[:, :channels], edge[:, channels:])
            for b in range(2):
                taps = jnp.concatenate(parts[b : b + 3], axis=1)
                lanes = slice(b * channels, (b + 1) * channels)
                result = conv_acc[r, rows, lanes] + jnp.dot(
                    taps, convw_ref[2 * r], preferred_element_type=F32
                )
                result = jnp.where(row < valid_rows, result, 0.0)
                for h in range(0, channels, 128):
                    out_buf[r, h // 128, pl.ds(c * 2 * CHUNK + b, CHUNK, 2), :] = result[
                        :, h : h + 128
                    ]
                stat_acc[0] += result.reshape(CHUNK // 8, 8, channels).sum(axis=0)

    @pl.loop(0, n)
    def _(f):
        for r, h in sides:
            store(f, r, h).start()

    unit = (4 * row_tokens * group_size)
    group_row = lax.broadcasted_iota(jnp.int32, (channels, channels), 0) // group_size
    group_col = lax.broadcasted_iota(jnp.int32, (channels, channels), 1) // group_size
    group_ones = (group_row == group_col).astype(F32)

    def group_total(part):
        sums = jnp.sum(part, axis=0, keepdims=True)
        return jnp.dot(
            jnp.broadcast_to(sums, (8, channels)),
            group_ones,
            precision=lax.Precision.HIGHEST,
            preferred_element_type=F32,
        )

    tile_sum = group_total(stat_acc[0])
    tile_mean = tile_sum[0:1, :] / (valid_ref[me] * unit).astype(F32)

    @pl.loop(0, 2 * chunks)
    def _(c):
        pixels = pl.ds(pl.multiple_of(c * CHUNK, CHUNK), CHUNK)
        row = lax.broadcasted_iota(jnp.int32, (CHUNK, 128), 0) + c * CHUNK
        for r, h in sides:
            lanes = slice(h * 128, (h + 1) * 128)
            off = jnp.where(row < 2 * valid_rows, out_buf[r, h, pixels, :] - tile_mean[:, lanes], 0.0)
            stat_acc[1, :, lanes] += (off * off).reshape(CHUNK // 8, 8, 128).sum(axis=0)

    tile_square = group_total(stat_acc[1])
    line = lax.broadcasted_iota(jnp.int32, (8, channels), 0)
    sent_stat[...] = jnp.where(line == 0, tile_sum, tile_square)

    @pl.loop(1, n)
    def _(s):
        stat_copy(s).start()

    all_stat[me] = sent_stat[...]

    @pl.loop(1, n)
    def _(s):
        stat_copy(s).wait_recv()

    def add_sum(t, carry):
        total, units = carry
        return total + all_stat[t, 0:1, :], units + valid_ref[t]

    total, units = lax.fori_loop(
        0, n, add_sum, (jnp.zeros((1, channels), F32), jnp.zeros((), jnp.int32))
    )
    total_count = units.astype(F32) * unit
    mean = total / total_count

    def add_square(t, square):
        size = (valid_ref[t] * unit).astype(F32)
        off = all_stat[t, 0:1, :] / size - mean
        return square + all_stat[t, 1:2, :] + size * (off * off)

    square = lax.fori_loop(0, n, add_square, jnp.zeros((1, channels), F32))
    scale = gain_ref[...] * lax.rsqrt(square / total_count + 1e-05)
    norm_ref[...] = jnp.where(
        line == 0, mean, jnp.where(line == 1, scale, valid_ref[me].astype(F32))
    )

    @pl.loop(0, n)
    def _(f):
        for r, h in sides:
            store(f, r, h).wait()

    @pl.loop(0, chunks)
    def _(c):
        @pl.when(me < n - 1)
        def _():
            down_copy(c).wait_send()

        @pl.when(me > 0)
        def _():
            up_copy(c).wait_send()

    @pl.loop(1, n)
    def _(s):
        tok_copy(lax.rem(me + s, n)).wait_send()
        stat_copy(s).wait_send()

    own_pass.wait_send()

    @pl.loop(1, n // 2)
    def _(k):
        state_copy(k).wait_send()
        state_pass(k).wait_send()


def local(
    tokens,
    qkv_weight,
    out_weight,
    conv_weight,
    norm_gain,
    norm_bias,
    group_map,
    token_order,
    valid_frames,
):
    n = lax.axis_size("tm")
    count, width = tokens.shape
    channels = conv_weight.shape[3]
    row_tokens = count // n
    chunks = count // CHUNK
    state_shape = (width // 128 * (width // HEADS) + 16, 128)
    anywhere = pl.BlockSpec(memory_space=pl.ANY)
    vmem = pl.BlockSpec(memory_space=pltpu.VMEM)
    smem = pl.BlockSpec(memory_space=pltpu.SMEM)
    dma = pltpu.SemaphoreType.DMA
    conv, norm = pl.pallas_call(
        functools.partial(mega, n),
        out_shape=(
            jax.ShapeDtypeStruct((n, 2, 2 * row_tokens, channels), F32),
            jax.ShapeDtypeStruct((8, channels), F32),
        ),
        in_specs=[anywhere] * 4 + [vmem, smem, vmem, smem],
        out_specs=(anywhere, vmem),
        scratch_shapes=[
            pltpu.VMEM((count, width), BF16),
            pltpu.VMEM((width, 3 * width), BF16),
            pltpu.VMEM((width, 4 * channels), BF16),
            pltpu.VMEM((3, 3 * channels, channels), BF16),
            pltpu.VMEM((n, row_tokens, width), BF16),
            pltpu.VMEM((n, row_tokens, width), BF16),
            pltpu.VMEM((width // BLOCK, BLOCK, BLOCK), F32),
            pltpu.VMEM((8, width), F32),
            pltpu.VMEM(state_shape, BF16),
            pltpu.VMEM((n,) + state_shape, BF16),
            pltpu.VMEM((n,) + state_shape, F32),
            pltpu.VMEM(state_shape, F32),
            pltpu.VMEM(state_shape, F32),
            pltpu.VMEM((CHUNK, width), F32),
            pltpu.VMEM((2, count, 4 * channels), BF16),
            pltpu.VMEM((2, count, 2 * channels), BF16),
            pltpu.VMEM((2, count, 2 * channels), F32),
            pltpu.VMEM((2, 8, channels), F32),
            pltpu.VMEM((8, channels), F32),
            pltpu.VMEM((n, 8, channels), F32),
            pltpu.VMEM((2, channels // 128, 2 * count, 128), F32),
            dma((4,)),
            dma((n,)),
            dma((n,)),
            dma((n // 2,)),
            dma((n // 2,)),
            dma((n // 2,)),
            dma((n // 2,)),
            dma((2, chunks)),
            dma((2, chunks)),
            dma((n,)),
            dma((n,)),
            dma((n, 2, channels // 128)),
        ],
        compiler_params=pltpu.CompilerParams(
            collective_id=0, has_side_effects=True, vmem_limit_bytes=60 * 1024 * 1024
        ),
    )(
        tokens,
        qkv_weight,
        out_weight,
        conv_weight.reshape(3, 3 * channels, channels),
        norm_gain[None],
        group_map,
        token_order[None],
        valid_frames,
    )
    frame = lax.broadcasted_iota(jnp.int32, conv.shape, 0).astype(F32)
    normed = (conv - norm[0]) * norm[1] + norm_bias
    return jnp.where(frame < norm[2], jax.nn.silu(normed), 0.0).astype(BF16)


def solution(mesh):
    in_specs = (P(("clip", "tm"), None), P(), P(), P(), P(), P(), P("clip"), P("clip"), P("clip"))
    out_specs = P("clip", "tm", None, None)
    return jax.shard_map(local, mesh=mesh, in_specs=in_specs, out_specs=out_specs, check_vma=False)
```
